32 devices in a mesh: head: 4 (over z), tok: 8 (over y, x, core).
Axes of the slice: x: 2, y: 2, z: 4, core: 2. Of those that a mesh axis runs over, the one named last changes fastest.
Arguments:
- video_q: bfloat16 [7168, 2048], P('tok', 'head'), may hold values from -6 to 6
- video_k: bfloat16 [7168, 2048], P('tok', 'head'), may hold values from -6 to 6
- video_v: bfloat16 [7168, 2048], P('tok', 'head'), may hold values from -6 to 6
- audio_q: bfloat16 [256, 2048], P('tok', 'head'), may hold values from -6 to 6
- audio_k: bfloat16 [256, 2048], P('tok', 'head'), may hold values from -6 to 6
- audio_v: bfloat16 [256, 2048], P('tok', 'head'), may hold values from -6 to 6
- norm_gain: float32 [2048], replicated, may hold values from 0.5 to 1.5
Outputs:
- video_out: bfloat16 [7168, 2048], P(('tok', 'head'))
- audio_out: bfloat16 [256, 2048], P('tok', 'head')
The draws below stay inside these ranges and needn't reach their ends.
All inputs are finite; a program needn't handle non-finite values.
Results may differ from the reference program's by a relative error of at most 0.0095.
Values may be sent and summed in bfloat16 or wider, within the bound.
No kernel may reach another device: no remote copies, remote signals or barrier semaphores. Data moves between devices by JAX's collectives and lax.ppermute only.
A program may use at most 64 MiB of HBM per device.

```python
import jax
import jax.numpy as jnp
from jax import lax

HEADS = 32
HEAD_DIM = 64
D = 2048
VTOK = 7168
ATOK = 256


def base_draw(key, salt, count):
    sub = jax.random.fold_in(key, salt)
    return jnp.clip(jax.random.normal(sub, (count, D), jnp.float32), -6.0, 6.0)


def query_draw(key, salt, count):
    values = base_draw(key, salt, count)
    return values


def key_draw(key, salt, count):
    values = base_draw(key, salt, count)
    return values


def draw_video_q(key, part):
    return query_draw(key, 11, VTOK).astype(jnp.bfloat16)


def draw_video_k(key, part):
    return key_draw(key, 12, VTOK).astype(jnp.bfloat16)


def draw_audio_q(key, part):
    return query_draw(key, 13, ATOK).astype(jnp.bfloat16)


def draw_audio_k(key, part):
    return key_draw(key, 14, ATOK).astype(jnp.bfloat16)


def level_of(rng, shape, pieces, low, top_value):
    loudness, own = 1.0, jax.random.fold_in(rng, 6)
    for position, parts in pieces:
        draws = jnp.exp(jax.random.uniform(jax.random.fold_in(own, position), (parts,), jnp.float32, low / len(pieces), top_value / len(pieces)))
        loudness = loudness * jnp.repeat(draws, shape[position] // parts).reshape([-1 if axis == position else 1 for axis in range(len(shape))])
    return loudness


def gaussian(key, dims, deviation, most, shards=(), held_as=jnp.bfloat16):
    factor_of = level_of(key, dims, shards, -0.22, 0.18) if shards else 1.0
    values = jax.random.normal(key, dims, jnp.float32) * deviation * factor_of
    return jnp.minimum(jnp.maximum(values, -most), most).astype(held_as)


def setup_inputs(seed: int = 0) -> dict:
    arg_keys = jax.random.split(jax.random.key(seed), 8)
    video_q = draw_video_q(jax.random.fold_in(arg_keys[7], 71), 0)
    video_k = draw_video_k(jax.random.fold_in(arg_keys[7], 71), 0)
    video_v = gaussian(arg_keys[2], (VTOK, D), 1.0, 6.0, ((0, 8), (1, 4)))
    audio_q = draw_audio_q(jax.random.fold_in(arg_keys[7], 71), 0)
    audio_k = draw_audio_k(jax.random.fold_in(arg_keys[7], 71), 0)
    audio_v = gaussian(arg_keys[5], (ATOK, D), 1.0, 6.0, ((0, 8), (1, 4)))
    norm_gain = jnp.clip(1.0 + 0.1 * jax.random.normal(arg_keys[6], (D,), jnp.float32), 0.5, 1.5)
    return dict(video_q=video_q, video_k=video_k, video_v=video_v, audio_q=audio_q, audio_k=audio_k, audio_v=audio_v, norm_gain=norm_gain)


def attend(query_part, key_part, value_part):
    scaling = HEAD_DIM ** (-0.5)

    def split_heads(matrix):
        return matrix.reshape(matrix.shape[0], HEADS, HEAD_DIM).transpose(1, 0, 2)

    def one_head(triple):
        query_head, key_head, value_head = triple
        scores = jnp.dot(query_head, key_head.T, preferred_element_type=jnp.float32) * scaling
        row_max = lax.optimization_barrier(jnp.max(scores, axis=1, keepdims=True))
        weights = jnp.exp(scores - row_max)
        row_sum = lax.optimization_barrier(jnp.sum(weights, axis=1, keepdims=True))
        result = jnp.dot(weights.astype(jnp.bfloat16), value_head, preferred_element_type=jnp.float32) / row_sum
        return result.astype(jnp.bfloat16)
    heads_out = lax.map(one_head, (split_heads(query_part), split_heads(key_part), split_heads(value_part)))
    return heads_out.transpose(1, 0, 2).reshape(query_part.shape[0], HEADS * HEAD_DIM)

def reference(video_q, video_k, video_v, audio_q, audio_k, audio_v, norm_gain):
    video_attn = attend(video_q, audio_k, audio_v)
    widened = video_attn.astype(jnp.float32)
    mean_square = lax.optimization_barrier(jnp.mean(widened * widened, axis=1, keepdims=True))
    video_out = (widened * lax.rsqrt(mean_square + 1e-06) * norm_gain).astype(jnp.bfloat16)
    audio_out = attend(audio_q, video_k, video_v)
    return (video_out, audio_out)
```

```python
import functools

import jax
import jax.numpy as jnp
from jax import lax
from jax.experimental import pallas as pl
from jax.experimental.pallas import tpu as pltpu
from jax.sharding import PartitionSpec as P


HEAD_DIM = 64
PAIR = 2 * HEAD_DIM
QUERY_BLOCK = 256
BF16, F32 = jnp.bfloat16, jnp.float32
VMEM = pl.BlockSpec(memory_space=pltpu.VMEM)


def partners(size):
    steps = sorted(range(1, size), key=lambda s: (-s.bit_length(), s))
    return steps if size & (size - 1) == 0 else list(range(1, size))


def peer(me, step, size):
    return me ^ step if size & (size - 1) == 0 else lax.rem(me + step, size)


def sender(me, step, size):
    return me ^ step if size & (size - 1) == 0 else lax.rem(me + size - step, size)


def exchange(x, axis, step):
    size = lax.axis_size(axis)
    pairs = [
        (i, i ^ step if size & (size - 1) == 0 else (i + step) % size)
        for i in range(size)
    ]
    return lax.ppermute(x, axis, pairs)


def columns(pair, base=0):
    return slice(base + pair * PAIR, base + (pair + 1) * PAIR)


def lane_halves(x):
    lane = lax.broadcasted_iota(jnp.int32, x.shape, 1)
    zero = jnp.zeros_like(x)
    return jnp.where(lane < HEAD_DIM, x, zero), jnp.where(lane < HEAD_DIM, zero, x)


def attend_pair(query, key, value, shift_of):
    scale = HEAD_DIM**-0.5
    weights, shifts = [], []
    for one in lane_halves(key):
        scores = lax.dot_general(
            query, one, (((1,), (1,)), ((), ())), preferred_element_type=F32
        )
        shift = shift_of(jnp.max(scores, axis=1, keepdims=True) * scale)
        weights.append(jnp.exp(scores * scale - shift).astype(BF16))
        shifts.append(shift)
    result = None
    for weight, v, one in zip(weights, lane_halves(value), lane_halves(jnp.ones_like(value))):
        part = jnp.dot(
            weight, jnp.concatenate([v, one], axis=1), preferred_element_type=F32
        )
        result = part if result is None else result + part
    return result[:, :PAIR], result[:, PAIR:], shifts


def video_kernel(query_ref, audio_ref, *out_refs, steps, axis, size):
    rows, width = out_refs[0].shape
    me = lax.axis_index(axis)
    for step, out_ref in zip(steps, out_refs):
        owner = me if step == 0 else peer(me, step, size)
        first = pl.multiple_of(owner * rows, rows)
        for pair in range(width // PAIR):
            out, total, _ = attend_pair(
                query_ref[pl.ds(first, rows), columns(pair)],
                audio_ref[:, columns(pair, width)],
                audio_ref[:, columns(pair, 2 * width)],
                lambda top: top,
            )
            out_ref[:, columns(pair)] = (out / total).astype(BF16)


def video_part(video_q, audio, steps, size):
    width = video_q.shape[1]
    rows, keys = video_q.shape[0] // size, audio.shape[0]
    work = rows * keys * width * len(steps)
    return pl.pallas_call(
        functools.partial(video_kernel, steps=steps, axis="head", size=size),
        out_shape=[jax.ShapeDtypeStruct((rows, width), BF16)] * len(steps),
        in_specs=[VMEM] * 2,
        out_specs=[VMEM] * len(steps),
        compiler_params=pltpu.CompilerParams(vmem_limit_bytes=16 << 20),
        cost_estimate=pl.CostEstimate(
            flops=4 * work,
            bytes_accessed=4 * rows * width * len(steps),
            transcendentals=work // HEAD_DIM,
        ),
        name="video_part",
    )(video_q, audio)


def round_up(top):
    return (top + jnp.abs(top) * 2.0**-8).astype(BF16).astype(F32)


def audio_kernel(audio_ref, key_ref, value_ref, out_ref):
    queries = audio_ref.shape[0]
    width = key_ref.shape[1]
    block = QUERY_BLOCK if queries % QUERY_BLOCK == 0 else queries

    def one_block(first):
        at = pl.ds(first, block)
        lane = lax.broadcasted_iota(jnp.int32, (block, PAIR), 1)
        tops = jnp.zeros((block, PAIR), F32)
        totals = jnp.zeros((block, PAIR), F32)
        for pair in range(width // PAIR):
            out, total, (low, high) = attend_pair(
                audio_ref[at, columns(pair)],
                key_ref[:, columns(pair)],
                value_ref[:, columns(pair)],
                round_up,
            )
            out_ref[at, columns(pair)] = out.astype(BF16)
            mine = (lane % HEAD_DIM) // 8 == pair
            tops = jnp.where(mine, jnp.where(lane < HEAD_DIM, low, high), tops)
            totals = jnp.where(mine, total, totals)
        coarse = totals.astype(BF16).astype(F32)
        kind = lane % 8
        stats = jnp.where(kind < 3, tops, jnp.where(kind < 6, coarse, totals - coarse))
        out_ref[at, pl.ds(width, PAIR)] = stats.astype(BF16)

    if block == queries:
        one_block(0)
    else:
        pl.loop(0, queries // block)(lambda i: one_block(pl.multiple_of(i * block, block)))


def audio_part(audio, video_k, video_v):
    queries = audio.shape[0]
    keys, width = video_k.shape
    assert width // PAIR <= 8
    return pl.pallas_call(
        audio_kernel,
        out_shape=jax.ShapeDtypeStruct((queries, width + PAIR), BF16),
        in_specs=[VMEM] * 3,
        out_specs=VMEM,
        compiler_params=pltpu.CompilerParams(vmem_limit_bytes=24 << 20),
        cost_estimate=pl.CostEstimate(
            flops=4 * queries * keys * width,
            bytes_accessed=4 * keys * width,
            transcendentals=queries * keys * width // HEAD_DIM,
        ),
        name="audio_part",
    )(audio, video_k, video_v)


def combine_kernel(part_ref, out_ref):
    shards, _, wide = part_ref.shape
    width = wide - PAIR
    at = lax.broadcasted_iota(jnp.int32, (PAIR, width), 0)
    head = lax.broadcasted_iota(jnp.int32, (PAIR, width), 1) // HEAD_DIM
    home = (head % 2) * HEAD_DIM + (head // 2) * 8
    pick_top = (at == home).astype(BF16)
    pick_total = ((at == home + 3) | (at == home + 6)).astype(BF16)
    stats = [part_ref[i, :, pl.ds(width, PAIR)] for i in range(shards)]
    tops = [jnp.dot(s, pick_top, preferred_element_type=F32) for s in stats]
    totals = [jnp.dot(s, pick_total, preferred_element_type=F32) for s in stats]
    top = functools.reduce(jnp.maximum, tops)
    total, out = 0.0, 0.0
    for i in range(shards):
        factor = jnp.exp(tops[i] - top)
        total = total + factor * totals[i]
        out = out + factor * part_ref[i, :, pl.ds(0, width)].astype(F32)
    out_ref[...] = (out / total).astype(BF16)


def combine(parts):
    _, rows, wide = parts.shape
    return pl.pallas_call(
        combine_kernel,
        out_shape=jax.ShapeDtypeStruct((rows, wide - PAIR), BF16),
        in_specs=[VMEM],
        out_specs=VMEM,
        compiler_params=pltpu.CompilerParams(vmem_limit_bytes=8 << 20),
        name="audio_combine",
    )(parts)


def norm_kernel(gain_ref, *refs, steps, axis, size):
    *part_refs, out_ref = refs
    _, width = part_refs[0].shape
    me = lax.axis_index(axis)
    square = 0.0
    for part_ref in part_refs:
        part = part_ref[...].astype(F32)
        square = square + jnp.sum(part * part, axis=1, keepdims=True)
    factor = lax.rsqrt(square / out_ref.shape[1] + 1e-06)
    for step, part_ref in zip(steps, part_refs):
        owner = me if step == 0 else sender(me, step, size)
        at = pl.ds(pl.multiple_of(owner * width, width), width)
        out_ref[:, at] = (part_ref[...].astype(F32) * factor * gain_ref[:, at]).astype(BF16)


def norm(gain, parts, steps, size):
    rows, width = parts[0].shape
    return pl.pallas_call(
        functools.partial(norm_kernel, steps=steps, axis="head", size=size),
        out_shape=jax.ShapeDtypeStruct((rows, width * size), BF16),
        in_specs=[VMEM] * (1 + len(parts)),
        out_specs=VMEM,
        compiler_params=pltpu.CompilerParams(vmem_limit_bytes=8 << 20),
        name="video_norm",
    )(gain.reshape(1, -1), *parts)


def attend_all(video_q, video_k, video_v, audio_q, audio_k, audio_v, norm_gain):
    heads, toks = lax.axis_size("head"), lax.axis_size("tok")
    own = jnp.concatenate([audio_q, audio_k, audio_v], axis=1)
    audio = lax.all_gather(own, "tok", axis=0, tiled=True)
    steps = partners(heads)
    received = []
    for step in steps:
        (piece,) = video_part(video_q, audio, (step,), heads)
        audio, piece = lax.optimization_barrier((audio, piece))
        received.append(exchange(piece, "head", step))
    (mine,) = video_part(video_q, audio, (0,), heads)
    audio, mine = lax.optimization_barrier((audio, mine))
    parts = audio_part(audio, video_k, video_v)
    parts = parts.reshape(toks, audio_q.shape[0], parts.shape[1])
    parts = lax.all_to_all(parts, "tok", split_axis=0, concat_axis=0, tiled=True)
    audio_out = combine(parts)
    video_out = norm(norm_gain, [mine, *received], [0, *steps], heads)
    return (video_out, audio_out)


def solution(mesh):
    placed = P("tok", "head")
    return jax.shard_map(
        attend_all,
        mesh=mesh,
        in_specs=(placed,) * 6 + (P(),),
        out_specs=(P(("tok", "head"), None), placed),
        check_vma=False,
    )
```

```python
import functools

import jax
import jax.numpy as jnp
from jax import lax
from jax.experimental import pallas as pl
from jax.experimental.pallas import tpu as pltpu
from jax.sharding import PartitionSpec as P


HEAD_DIM = 64
PAIR = 2 * HEAD_DIM
QUERY_BLOCK = 256
DIRECT_LIMIT = 8
BF16, F32 = jnp.bfloat16, jnp.float32
VMEM = pl.BlockSpec(memory_space=pltpu.VMEM)


def partners(size):
    steps = sorted(range(1, size), key=lambda s: (-s.bit_length(), s))
    return steps if size & (size - 1) == 0 else list(range(1, size))


def peer(me, step, size):
    return me ^ step if size & (size - 1) == 0 else lax.rem(me + step, size)


def sender(me, step, size):
    return me ^ step if size & (size - 1) == 0 else lax.rem(me + size - step, size)


def exchange(x, axis, step):
    size = lax.axis_size(axis)
    pairs = [
        (i, i ^ step if size & (size - 1) == 0 else (i + step) % size)
        for i in range(size)
    ]
    return lax.ppermute(x, axis, pairs)


def columns(pair, base=0):
    return slice(base + pair * PAIR, base + (pair + 1) * PAIR)


def lane_halves(x):
    lane = lax.broadcasted_iota(jnp.int32, x.shape, 1)
    zero = jnp.zeros_like(x)
    return jnp.where(lane < HEAD_DIM, x, zero), jnp.where(lane < HEAD_DIM, zero, x)


def attend_pair(query, key, value, shift_of):
    scale = HEAD_DIM**-0.5
    weights, shifts = [], []
    for one in lane_halves(key):
        scores = lax.dot_general(
            query, one, (((1,), (1,)), ((), ())), preferred_element_type=F32
        )
        shift = shift_of(jnp.max(scores, axis=1, keepdims=True) * scale)
        weights.append(jnp.exp(scores * scale - shift).astype(BF16))
        shifts.append(shift)
    result = None
    for weight, v, one in zip(weights, lane_halves(value), lane_halves(jnp.ones_like(value))):
        part = jnp.dot(
            weight, jnp.concatenate([v, one], axis=1), preferred_element_type=F32
        )
        result = part if result is None else result + part
    return result[:, :PAIR], result[:, PAIR:], shifts


def copy_all(pairs, sems):
    copies = [
        pltpu.make_async_copy(source, target, sems.at[i])
        for i, (source, target) in enumerate(pairs)
    ]
    for copy in copies:
        copy.start()
    for copy in copies:
        copy.wait()


def pack_kernel(*refs):
    *part_refs, own_ref, sems = refs
    width = part_refs[0].shape[1]
    spots = [own_ref.at[:, pl.ds(i * width, width)] for i in range(len(part_refs))]
    copy_all(zip(part_refs, spots), sems)


def pack(parts):
    rows, width = parts[0].shape
    return pl.pallas_call(
        pack_kernel,
        out_shape=pltpu.VMEM((rows, len(parts) * width), BF16),
        in_specs=[pl.BlockSpec(memory_space=pltpu.HBM)] * len(parts),
        out_specs=VMEM,
        scratch_shapes=[pltpu.SemaphoreType.DMA((len(parts),))],
        compiler_params=pltpu.CompilerParams(vmem_limit_bytes=8 << 20),
    )(*(pltpu.with_memory_space_constraint(x, pltpu.HBM) for x in parts))


def stacked(refs, at):
    return jnp.concatenate([ref[:, at] for ref in refs], axis=0)


def video_kernel(query_ref, *refs, step, axis, size):
    *piece_refs, out_ref = refs
    rows, width = out_ref.shape
    me = lax.axis_index(axis)
    owner = me if step == 0 else peer(me, step, size)
    first = pl.multiple_of(owner * rows, rows)
    for pair in range(width // PAIR):
        out, total, _ = attend_pair(
            query_ref[pl.ds(first, rows), columns(pair)],
            stacked(piece_refs, columns(pair, width)),
            stacked(piece_refs, columns(pair, 2 * width)),
            lambda top: top,
        )
        out_ref[:, columns(pair)] = (out / total).astype(BF16)


def video_part(query, pieces, step, size):
    rows = query.shape[0] // size
    width = query.shape[1]
    work = rows * sum(piece.shape[0] for piece in pieces) * width
    return pl.pallas_call(
        functools.partial(video_kernel, step=step, axis="head", size=size),
        out_shape=pltpu.VMEM((rows, width), BF16),
        in_specs=[VMEM] * (1 + len(pieces)),
        out_specs=VMEM,
        compiler_params=pltpu.CompilerParams(vmem_limit_bytes=16 << 20),
        cost_estimate=pl.CostEstimate(
            flops=4 * work,
            bytes_accessed=4 * rows * width,
            transcendentals=work // HEAD_DIM,
        ),
        name="video_part",
    )(query, *pieces)


def round_up(top):
    return (top + jnp.abs(top) * 2.0**-8).astype(BF16).astype(F32)


def audio_kernel(*refs, pieces, offsets, axis, size):
    piece_refs, (key_ref, value_ref, out_ref) = refs[:pieces], refs[pieces:]
    rows = out_ref.shape[1]
    width = key_ref.shape[1]
    queries = sum(ref.shape[0] for ref in piece_refs)
    block = queries
    if pieces == 1 and queries % QUERY_BLOCK == 0 and QUERY_BLOCK % rows == 0:
        block = QUERY_BLOCK

    def put(first, at, value):
        value = value.astype(BF16)
        for i in range(block // rows):
            if offsets is None:
                owner = first // rows + i
            else:
                owner = peer(lax.axis_index(axis), offsets[i], size)
            out_ref[owner, :, at] = value[i * rows : (i + 1) * rows]

    def one_block(first):
        lane = lax.broadcasted_iota(jnp.int32, (block, PAIR), 1)
        tops = jnp.zeros((block, PAIR), F32)
        totals = jnp.zeros((block, PAIR), F32)
        for pair in range(width // PAIR):
            if pieces == 1:
                query = piece_refs[0][pl.ds(first, block), columns(pair)]
            else:
                query = stacked(piece_refs, columns(pair))
            out, total, (low, high) = attend_pair(
                query, key_ref[:, columns(pair)], value_ref[:, columns(pair)], round_up
            )
            put(first, columns(pair), out)
            mine = (lane % HEAD_DIM) // 8 == pair
            tops = jnp.where(mine, jnp.where(lane < HEAD_DIM, low, high), tops)
            totals = jnp.where(mine, total, totals)
        coarse = totals.astype(BF16).astype(F32)
        kind = lane % 8
        stats = jnp.where(kind < 3, tops, jnp.where(kind < 6, coarse, totals - coarse))
        put(first, slice(width, width + PAIR), stats)

    if block == queries:
        one_block(0)
    else:
        pl.loop(0, queries // block)(lambda i: one_block(pl.multiple_of(i * block, block)))


def audio_part(pieces, offsets, video_k, video_v, rows, size):
    keys, width = video_k.shape
    work = rows * size * keys * width
    assert width // PAIR <= 8
    return pl.pallas_call(
        functools.partial(
            audio_kernel, pieces=len(pieces), offsets=offsets, axis="tok", size=size
        ),
        out_shape=pltpu.VMEM((size, rows, width + PAIR), BF16),
        in_specs=[VMEM] * (2 + len(pieces)),
        out_specs=VMEM,
        compiler_params=pltpu.CompilerParams(vmem_limit_bytes=24 << 20),
        cost_estimate=pl.CostEstimate(
            flops=4 * work,
            bytes_accessed=4 * keys * width,
            transcendentals=work // HEAD_DIM,
        ),
        name="audio_part",
    )(*pieces, video_k, video_v)


def combine_kernel(part_ref, out_ref):
    shards, _, wide = part_ref.shape
    width = wide - PAIR
    at = lax.broadcasted_iota(jnp.int32, (PAIR, width), 0)
    head = lax.broadcasted_iota(jnp.int32, (PAIR, width), 1) // HEAD_DIM
    home = (head % 2) * HEAD_DIM + (head // 2) * 8
    pick_top = (at == home).astype(BF16)
    pick_total = ((at == home + 3) | (at == home + 6)).astype(BF16)
    stats = [part_ref[i, :, pl.ds(width, PAIR)] for i in range(shards)]
    tops = [jnp.dot(s, pick_top, preferred_element_type=F32) for s in stats]
    totals = [jnp.dot(s, pick_total, preferred_element_type=F32) for s in stats]
    top = functools.reduce(jnp.maximum, tops)
    total, out = 0.0, 0.0
    for i in range(shards):
        factor = jnp.exp(tops[i] - top)
        total = total + factor * totals[i]
        out = out + factor * part_ref[i, :, pl.ds(0, width)].astype(F32)
    out_ref[...] = (out / total).astype(BF16)


def combine(parts):
    _, rows, wide = parts.shape
    return pl.pallas_call(
        combine_kernel,
        out_shape=jax.ShapeDtypeStruct((rows, wide - PAIR), BF16),
        in_specs=[VMEM],
        out_specs=VMEM,
        compiler_params=pltpu.CompilerParams(vmem_limit_bytes=8 << 20),
        name="audio_combine",
    )(parts)


def norm_kernel(gain_ref, *refs, steps, axis, size):
    *part_refs, out_ref = refs
    _, width = part_refs[0].shape
    me = lax.axis_index(axis)
    square = 0.0
    for part_ref in part_refs:
        part = part_ref[...].astype(F32)
        square = square + jnp.sum(part * part, axis=1, keepdims=True)
    factor = lax.rsqrt(square / out_ref.shape[1] + 1e-06)
    for step, part_ref in zip(steps, part_refs):
        owner = me if step == 0 else sender(me, step, size)
        at = pl.ds(pl.multiple_of(owner * width, width), width)
        out_ref[:, at] = (part_ref[...].astype(F32) * factor * gain_ref[:, at]).astype(BF16)


def norm(gain, parts, steps, size):
    rows, width = parts[0].shape
    return pl.pallas_call(
        functools.partial(norm_kernel, steps=steps, axis="head", size=size),
        out_shape=jax.ShapeDtypeStruct((rows, width * size), BF16),
        in_specs=[VMEM] * (1 + len(parts)),
        out_specs=VMEM,
        compiler_params=pltpu.CompilerParams(vmem_limit_bytes=8 << 20),
        name="video_norm",
    )(gain.reshape(1, -1), *parts)


def is_direct(size):
    return size & (size - 1) == 0 and 2 <= size <= DIRECT_LIMIT


def gather(x, axis):
    size = lax.axis_size(axis)
    if not is_direct(size):
        return [lax.all_gather(x, axis, axis=0, tiled=True)], None
    pieces = {0: x}
    out, beside = gather_steps(size)
    for step in out:
        pieces[step] = exchange(x, axis, step)
    for step in beside:
        pieces[step] = exchange(pieces[step - 1], axis, 1)
    return list(pieces.values()), list(pieces)


def attend_all(video_q, video_k, video_v, audio_q, audio_k, audio_v, norm_gain):
    heads, toks = lax.axis_size("head"), lax.axis_size("tok")
    audio_rows = audio_q.shape[0]
    steps = partners(heads)

    own = pack([audio_q, audio_k, audio_v])
    pieces, offsets = gather(own, "tok")
    video_q = pack([video_q])

    received = []
    for step in steps:
        piece = video_part(video_q, pieces, step, heads)
        received.append(exchange(piece, "head", step))
    mine = video_part(video_q, pieces, 0, heads)
    parts = audio_part(pieces, offsets, video_k, video_v, audio_rows, toks)
    parts = lax.all_to_all(parts, "tok", split_axis=0, concat_axis=0, tiled=True)
    audio_out = combine(parts)
    video_out = norm(norm_gain, [mine, *received], [0, *steps], heads)
    return (video_out, audio_out)


def gather_steps(size):
    steps = sorted(range(2, size, 2), key=lambda s: (-s.bit_count(), -s))
    return [*steps, 1], [s + 1 for s in steps]


def solution(mesh):
    placed = P("tok", "head")
    return jax.shard_map(
        attend_all,
        mesh=mesh,
        in_specs=(placed,) * 6 + (P(),),
        out_specs=(P(("tok", "head"), None), placed),
        check_vma=False,
    )
```

```python
import functools

import jax
import jax.numpy as jnp
from jax import lax
from jax.experimental import pallas as pl
from jax.experimental.pallas import tpu as pltpu
from jax.sharding import PartitionSpec as P


HEAD_DIM = 64
PAIR = 2 * HEAD_DIM
QUERY_BLOCK = 256
DIRECT_LIMIT = 8
BF16, F32 = jnp.bfloat16, jnp.float32
VMEM = pl.BlockSpec(memory_space=pltpu.VMEM)


def partners(size):
    steps = sorted(range(1, size), key=lambda s: (-s.bit_length(), s))
    return steps if size & (size - 1) == 0 else list(range(1, size))


def peer(me, step, size):
    return me ^ step if size & (size - 1) == 0 else lax.rem(me + step, size)


def sender(me, step, size):
    return me ^ step if size & (size - 1) == 0 else lax.rem(me + size - step, size)


def exchange(x, axis, step):
    size = lax.axis_size(axis)
    pairs = [
        (i, i ^ step if size & (size - 1) == 0 else (i + step) % size)
        for i in range(size)
    ]
    return lax.ppermute(x, axis, pairs)


def columns(pair, base=0):
    return slice(base + pair * PAIR, base + (pair + 1) * PAIR)


def lane_halves(x):
    lane = lax.broadcasted_iota(jnp.int32, x.shape, 1)
    zero = jnp.zeros_like(x)
    return jnp.where(lane < HEAD_DIM, x, zero), jnp.where(lane < HEAD_DIM, zero, x)


def attend_pair(query, key, value, shift_of):
    scale = HEAD_DIM**-0.5
    weights, shifts = [], []
    for one in lane_halves(key):
        scores = lax.dot_general(
            query, one, (((1,), (1,)), ((), ())), preferred_element_type=F32
        )
        shift = shift_of(jnp.max(scores, axis=1, keepdims=True) * scale)
        weights.append(jnp.exp(scores * scale - shift).astype(BF16))
        shifts.append(shift)
    result = None
    for weight, v, one in zip(weights, lane_halves(value), lane_halves(jnp.ones_like(value))):
        part = jnp.dot(
            weight, jnp.concatenate([v, one], axis=1), preferred_element_type=F32
        )
        result = part if result is None else result + part
    return result[:, :PAIR], result[:, PAIR:], shifts


def copy_all(pairs, sems):
    copies = [
        pltpu.make_async_copy(source, target, sems.at[i])
        for i, (source, target) in enumerate(pairs)
    ]
    for copy in copies:
        copy.start()
    for copy in copies:
        copy.wait()


def pack_kernel(*refs):
    *part_refs, own_ref, sems = refs
    width = part_refs[0].shape[1]
    spots = [own_ref.at[:, pl.ds(i * width, width)] for i in range(len(part_refs))]
    copy_all(zip(part_refs, spots), sems)


def pack(parts):
    rows, width = parts[0].shape
    return pl.pallas_call(
        pack_kernel,
        out_shape=pltpu.VMEM((rows, len(parts) * width), BF16),
        in_specs=[pl.BlockSpec(memory_space=pltpu.HBM)] * len(parts),
        out_specs=VMEM,
        scratch_shapes=[pltpu.SemaphoreType.DMA((len(parts),))],
        compiler_params=pltpu.CompilerParams(vmem_limit_bytes=8 << 20),
    )(*(pltpu.with_memory_space_constraint(x, pltpu.HBM) for x in parts))


def stacked(refs, at):
    return jnp.concatenate([ref[:, at] for ref in refs], axis=0)


def video_kernel(query_ref, *refs, step, axis, size):
    *piece_refs, out_ref = refs
    rows, width = out_ref.shape
    me = lax.axis_index(axis)
    owner = me if step == 0 else peer(me, step, size)
    first = pl.multiple_of(owner * rows, rows)
    for pair in range(width // PAIR):
        out, total, _ = attend_pair(
            query_ref[pl.ds(first, rows), columns(pair)],
            stacked(piece_refs, columns(pair, width)),
            stacked(piece_refs, columns(pair, 2 * width)),
            lambda top: top,
        )
        out_ref[:, columns(pair)] = (out / total).astype(BF16)


def video_part(query, pieces, step, size):
    rows = query.shape[0] // size
    width = query.shape[1]
    work = rows * sum(piece.shape[0] for piece in pieces) * width
    return pl.pallas_call(
        functools.partial(video_kernel, step=step, axis="head", size=size),
        out_shape=pltpu.VMEM((rows, width), BF16),
        in_specs=[VMEM] * (1 + len(pieces)),
        out_specs=VMEM,
        compiler_params=pltpu.CompilerParams(vmem_limit_bytes=16 << 20),
        cost_estimate=pl.CostEstimate(
            flops=4 * work,
            bytes_accessed=4 * rows * width,
            transcendentals=work // HEAD_DIM,
        ),
        name="video_part",
    )(query, *pieces)


def round_up(top):
    return (top + jnp.abs(top) * 2.0**-8).astype(BF16).astype(F32)


def statistics(tops, totals):
    lane = lax.broadcasted_iota(jnp.int32, tops[0].shape, 1)
    top, total = jnp.zeros(lane.shape, F32), jnp.zeros(lane.shape, F32)
    for pair in range(len(tops)):
        mine = (lane % HEAD_DIM) // 8 == pair
        top = jnp.where(mine, tops[pair], top)
        total = jnp.where(mine, totals[pair], total)
    coarse = total.astype(BF16).astype(F32)
    kind = lane % 8
    return jnp.where(kind < 3, top, jnp.where(kind < 6, coarse, total - coarse))


def audio_kernel(*refs, pieces, offsets):
    piece_refs, (key_ref, value_ref, *out_refs) = refs[:pieces], refs[pieces:]
    rows = out_refs[0].shape[1]
    width = key_ref.shape[1]
    queries = sum(ref.shape[0] for ref in piece_refs)
    block = queries
    if pieces == 1 and queries % QUERY_BLOCK == 0 and QUERY_BLOCK % rows == 0:
        block = QUERY_BLOCK

    def put(first, at, value):
        value = value.astype(BF16)
        for i in range(block // rows):
            if offsets is None:
                target = out_refs[0].at[first // rows + i]
            else:
                target = out_refs[offsets[i] % 2].at[offsets[i] // 2]
            target[:, at] = value[i * rows : (i + 1) * rows]

    def one_block(first):
        tops, totals = [], []
        for pair in range(width // PAIR):
            if pieces == 1:
                query = piece_refs[0][pl.ds(first, block), columns(pair)]
            else:
                query = stacked(piece_refs, columns(pair))
            out, total, (low, high) = attend_pair(
                query, key_ref[:, columns(pair)], value_ref[:, columns(pair)], round_up
            )
            put(first, columns(pair), out)
            lane = lax.broadcasted_iota(jnp.int32, (block, PAIR), 1)
            tops.append(jnp.where(lane < HEAD_DIM, low, high))
            totals.append(total)
        put(first, slice(width, width + PAIR), statistics(tops, totals))

    if block == queries:
        one_block(0)
    else:
        pl.loop(0, queries // block)(lambda i: one_block(pl.multiple_of(i * block, block)))


def audio_part(pieces, offsets, video_k, video_v, rows, size):
    keys, width = video_k.shape
    work = rows * size * keys * width
    assert width // PAIR <= 8
    shapes = [(size, rows, width + PAIR)] if offsets is None else [(size // 2, rows, width + PAIR)] * 2
    return pl.pallas_call(
        functools.partial(audio_kernel, pieces=len(pieces), offsets=offsets),
        out_shape=[pltpu.VMEM(shape, BF16) for shape in shapes],
        in_specs=[VMEM] * (2 + len(pieces)),
        out_specs=[VMEM] * len(shapes),
        compiler_params=pltpu.CompilerParams(vmem_limit_bytes=24 << 20),
        cost_estimate=pl.CostEstimate(
            flops=4 * work,
            bytes_accessed=4 * keys * width,
            transcendentals=work // HEAD_DIM,
        ),
        name="audio_part",
    )(*pieces, video_k, video_v)


def joined(part_refs):
    width = part_refs[0].shape[1] - PAIR
    at = lax.broadcasted_iota(jnp.int32, (PAIR, width), 0)
    head = lax.broadcasted_iota(jnp.int32, (PAIR, width), 1) // HEAD_DIM
    home = (head % 2) * HEAD_DIM + (head // 2) * 8
    pick_top = (at == home).astype(BF16)
    pick_total = ((at == home + 3) | (at == home + 6)).astype(BF16)
    stats = [ref[:, pl.ds(width, PAIR)] for ref in part_refs]
    tops = [jnp.dot(s, pick_top, preferred_element_type=F32) for s in stats]
    totals = [jnp.dot(s, pick_total, preferred_element_type=F32) for s in stats]
    top = functools.reduce(jnp.maximum, tops)
    total, out = 0.0, 0.0
    for i, ref in enumerate(part_refs):
        factor = jnp.exp(tops[i] - top)
        total = total + factor * totals[i]
        out = out + factor * ref[:, pl.ds(0, width)].astype(F32)
    return out, total, top


def merge_kernel(mine_ref, theirs_ref, *out_refs):
    for i, out_ref in enumerate(out_refs):
        out, total, top = joined([mine_ref.at[i], theirs_ref.at[i]])
        width = out.shape[1]
        out_ref[:, pl.ds(0, width)] = out.astype(BF16)
        pairs = [columns(pair) for pair in range(width // PAIR)]
        stats = statistics([top[:, at] for at in pairs], [total[:, at] for at in pairs])
        out_ref[:, pl.ds(width, PAIR)] = stats.astype(BF16)


def merge(mine, theirs):
    owners, rows, wide = mine.shape
    return pl.pallas_call(
        merge_kernel,
        out_shape=[pltpu.VMEM((rows, wide), BF16)] * owners,
        in_specs=[VMEM] * 2,
        out_specs=[VMEM] * owners,
        compiler_params=pltpu.CompilerParams(vmem_limit_bytes=8 << 20),
        name="audio_merge",
    )(mine, theirs)


def combine_kernel(*refs):
    *part_refs, out_ref = refs
    if len(part_refs[0].shape) == 3:
        part_refs = [part_refs[0].at[i] for i in range(part_refs[0].shape[0])]
    out, total, _ = joined(part_refs)
    out_ref[...] = (out / total).astype(BF16)


def combine(parts):
    rows, wide = parts[0].shape[-2:]
    return pl.pallas_call(
        combine_kernel,
        out_shape=jax.ShapeDtypeStruct((rows, wide - PAIR), BF16),
        in_specs=[VMEM] * len(parts),
        out_specs=VMEM,
        compiler_params=pltpu.CompilerParams(vmem_limit_bytes=8 << 20),
        name="audio_combine",
    )(*parts)


def norm_kernel(gain_ref, *refs, steps, axis, size):
    *part_refs, out_ref, done_ref, sems = refs
    rows, width = part_refs[0].shape
    me = lax.axis_index(axis)
    block = rows // sems.shape[0]
    copies = []
    for i in range(rows // block):
        here = pl.ds(i * block, block)
        square = 0.0
        for part_ref in part_refs:
            part = part_ref[here, :].astype(F32)
            square = square + jnp.sum(part * part, axis=1, keepdims=True)
        factor = lax.rsqrt(square / out_ref.shape[1] + 1e-06)
        for step, part_ref in zip(steps, part_refs):
            owner = me if step == 0 else sender(me, step, size)
            at = pl.ds(pl.multiple_of(owner * width, width), width)
            part = part_ref[here, :].astype(F32)
            done_ref[here, at] = (part * factor * gain_ref[:, at]).astype(BF16)
        copies.append(pltpu.make_async_copy(done_ref.at[here], out_ref.at[here], sems.at[i]))
        copies[-1].start()
    for copy in copies:
        copy.wait()


def norm(gain, parts, steps, size):
    rows, width = parts[0].shape
    blocks = next(n for n in (7, 4, 2, 1) if rows % (16 * n) == 0 or n == 1)
    return pl.pallas_call(
        functools.partial(norm_kernel, steps=steps, axis="head", size=size),
        out_shape=jax.ShapeDtypeStruct((rows, width * size), BF16),
        in_specs=[VMEM] * (1 + len(parts)),
        out_specs=pl.BlockSpec(memory_space=pltpu.HBM),
        scratch_shapes=[
            pltpu.VMEM((rows, width * size), BF16),
            pltpu.SemaphoreType.DMA((blocks,)),
        ],
        compiler_params=pltpu.CompilerParams(vmem_limit_bytes=8 << 20),
        name="video_norm",
    )(gain.reshape(1, -1), *parts)


def is_direct(size):
    return size & (size - 1) == 0 and 2 <= size <= DIRECT_LIMIT


def gather(x, axis):
    size = lax.axis_size(axis)
    if not is_direct(size):
        return [lax.all_gather(x, axis, axis=0, tiled=True)], None
    pieces = {0: x}
    out, beside = gather_steps(size)
    for step in out:
        pieces[step] = exchange(x, axis, step)
    for step in beside:
        pieces[step] = exchange(pieces[step - 1], axis, 1)
    return list(pieces.values()), list(pieces)


def attend_all(video_q, video_k, video_v, audio_q, audio_k, audio_v, norm_gain):
    heads, toks = lax.axis_size("head"), lax.axis_size("tok")
    audio_rows = audio_q.shape[0]
    steps = partners(heads)

    own = pack([audio_q, audio_k, audio_v])
    pieces, offsets = gather(own, "tok")
    video_q = pack([video_q])

    received = []
    for step in steps:
        piece = video_part(video_q, pieces, step, heads)
        received.append(exchange(piece, "head", step))
    mine = video_part(video_q, pieces, 0, heads)
    parts = audio_part(pieces, offsets, video_k, video_v, audio_rows, toks)
    if offsets is None:
        parts = lax.all_to_all(parts[0], "tok", split_axis=0, concat_axis=0, tiled=True)
        parts = [parts]
    else:
        theirs = exchange(parts[1], "tok", 1)
        merged = merge(parts[0], theirs)
        parts = list(merged[:1])
        for step in gather_steps(toks)[0][:-1]:
            parts.append(exchange(merged[step // 2], "tok", step))
    audio_out = combine(parts)
    video_out = norm(norm_gain, [mine, *received], [0, *steps], heads)
    return (video_out, audio_out)


def gather_steps(size):
    steps = sorted(range(2, size, 2), key=lambda s: (-s.bit_count(), -s))
    return [*steps, 1], [s + 1 for s in steps]


def solution(mesh):
    placed = P("tok", "head")
    return jax.shard_map(
        attend_all,
        mesh=mesh,
        in_specs=(placed,) * 6 + (P(),),
        out_specs=(P(("tok", "head"), None), placed),
        check_vma=False,
    )
```

```python
import functools

import jax
import jax.numpy as jnp
from jax import lax
from jax.experimental import pallas as pl
from jax.experimental.pallas import tpu as pltpu
from jax.sharding import PartitionSpec as P


HEAD_DIM = 64
PAIR = 2 * HEAD_DIM
QUERY_BLOCK = 256
DIRECT_LIMIT = 8
BF16, F32 = jnp.bfloat16, jnp.float32
VMEM = pl.BlockSpec(memory_space=pltpu.VMEM)


def partners(size):
    steps = sorted(range(1, size), key=lambda s: (-s.bit_length(), s))
    return steps if size & (size - 1) == 0 else list(range(1, size))


def peer(me, step, size):
    return me ^ step if size & (size - 1) == 0 else lax.rem(me + step, size)


def sender(me, step, size):
    return me ^ step if size & (size - 1) == 0 else lax.rem(me + size - step, size)


def exchange(x, axis, step):
    size = lax.axis_size(axis)
    pairs = [
        (i, i ^ step if size & (size - 1) == 0 else (i + step) % size)
        for i in range(size)
    ]
    return lax.ppermute(x, axis, pairs)


def columns(pair, base=0):
    return slice(base + pair * PAIR, base + (pair + 1) * PAIR)


def lane_halves(x):
    lane = lax.broadcasted_iota(jnp.int32, x.shape, 1)
    zero = jnp.zeros_like(x)
    return jnp.where(lane < HEAD_DIM, x, zero), jnp.where(lane < HEAD_DIM, zero, x)


def attend_pair(query, key, value, shift_of):
    scale = HEAD_DIM**-0.5
    weights, shifts = [], []
    for one in lane_halves(key):
        scores = lax.dot_general(
            query, one, (((1,), (1,)), ((), ())), preferred_element_type=F32
        )
        shift = shift_of(jnp.max(scores, axis=1, keepdims=True) * scale)
        weights.append(jnp.exp(scores * scale - shift).astype(BF16))
        shifts.append(shift)
    result = None
    for weight, v, one in zip(weights, lane_halves(value), lane_halves(jnp.ones_like(value))):
        part = jnp.dot(
            weight, jnp.concatenate([v, one], axis=1), preferred_element_type=F32
        )
        result = part if result is None else result + part
    return result[:, :PAIR], result[:, PAIR:], shifts


def copy_all(pairs, sems):
    copies = [
        pltpu.make_async_copy(source, target, sems.at[i])
        for i, (source, target) in enumerate(pairs)
    ]
    for copy in copies:
        copy.start()
    for copy in copies:
        copy.wait()


def pack_kernel(q_ref, k_ref, v_ref, own_ref, keys_ref, sems):
    width = k_ref.shape[1]
    spots = [(own_ref, 0, q_ref), (own_ref, 1, k_ref), (own_ref, 2, v_ref)]
    spots += [(keys_ref, 0, k_ref), (keys_ref, 1, v_ref)]
    copy_all(
        [(part, target.at[:, pl.ds(i * width, width)]) for target, i, part in spots], sems
    )


def in_hbm(*arrays):
    return [pltpu.with_memory_space_constraint(x, pltpu.HBM) for x in arrays]


def pack(audio_q, audio_k, audio_v):
    rows, width = audio_q.shape
    return pl.pallas_call(
        pack_kernel,
        out_shape=[pltpu.VMEM((rows, n * width), BF16) for n in (3, 2)],
        in_specs=[pl.BlockSpec(memory_space=pltpu.HBM)] * 3,
        out_specs=[VMEM] * 2,
        scratch_shapes=[pltpu.SemaphoreType.DMA((5,))],
        compiler_params=pltpu.CompilerParams(vmem_limit_bytes=8 << 20),
        name="pack",
    )(*in_hbm(audio_q, audio_k, audio_v))


def stage_kernel(video_ref, all_ref, block_ref, sems, *, step, size):
    rows = block_ref.shape[0]
    first = pl.multiple_of(peer(lax.axis_index("head"), step, size) * rows, rows)
    copy_all([(video_ref.at[pl.ds(first, rows)], block_ref), (video_ref, all_ref)], sems)


def stage(video_q, step, size):
    rows, width = video_q.shape
    return pl.pallas_call(
        functools.partial(stage_kernel, step=step, size=size),
        out_shape=[pltpu.VMEM((rows, width), BF16), pltpu.VMEM((rows // size, width), BF16)],
        in_specs=[pl.BlockSpec(memory_space=pltpu.HBM)],
        out_specs=[VMEM] * 2,
        scratch_shapes=[pltpu.SemaphoreType.DMA((2,))],
        compiler_params=pltpu.CompilerParams(vmem_limit_bytes=8 << 20),
        name="stage",
    )(*in_hbm(video_q))


def stacked(refs, at):
    return jnp.concatenate([ref[:, at] for ref in refs], axis=0)


def video_kernel(query_ref, *refs, step, axis, size, base):
    *piece_refs, out_ref = refs
    rows, width = out_ref.shape
    first = 0
    if query_ref.shape[0] != rows:
        me = lax.axis_index(axis)
        owner = me if step == 0 else peer(me, step, size)
        first = pl.multiple_of(owner * rows, rows)
    for pair in range(width // PAIR):
        out, total, _ = attend_pair(
            query_ref[pl.ds(first, rows), columns(pair)],
            stacked(piece_refs, columns(pair, base)),
            stacked(piece_refs, columns(pair, base + width)),
            lambda top: top,
        )
        out_ref[:, columns(pair)] = (out / total).astype(BF16)


def video_part(query, pieces, rows, step, size):
    width = query.shape[1]
    base = pieces[0].shape[1] - 2 * width
    work = rows * sum(piece.shape[0] for piece in pieces) * width
    return pl.pallas_call(
        functools.partial(
            video_kernel, step=step, axis="head", size=size, base=base
        ),
        out_shape=pltpu.VMEM((rows, width), BF16),
        in_specs=[VMEM] * (1 + len(pieces)),
        out_specs=VMEM,
        compiler_params=pltpu.CompilerParams(vmem_limit_bytes=16 << 20),
        cost_estimate=pl.CostEstimate(
            flops=4 * work,
            bytes_accessed=4 * rows * width,
            transcendentals=work // HEAD_DIM,
        ),
        name="video_part",
    )(query, *pieces)


def round_up(top):
    return (top + jnp.abs(top) * 2.0**-8).astype(BF16).astype(F32)


def statistics(tops, totals):
    lane = lax.broadcasted_iota(jnp.int32, tops[0].shape, 1)
    top, total = jnp.zeros(lane.shape, F32), jnp.zeros(lane.shape, F32)
    for pair in range(len(tops)):
        mine = (lane % HEAD_DIM) // 8 == pair
        top = jnp.where(mine, tops[pair], top)
        total = jnp.where(mine, totals[pair], total)
    coarse = total.astype(BF16).astype(F32)
    kind = lane % 8
    return jnp.where(kind < 3, top, jnp.where(kind < 6, coarse, total - coarse))


def audio_kernel(*refs, pieces, offsets):
    piece_refs, (key_ref, value_ref, *out_refs) = refs[:pieces], refs[pieces:]
    rows = out_refs[0].shape[1]
    width = key_ref.shape[1]
    queries = sum(ref.shape[0] for ref in piece_refs)
    block = queries
    if pieces == 1 and queries % QUERY_BLOCK == 0 and QUERY_BLOCK % rows == 0:
        block = QUERY_BLOCK

    def put(first, at, value):
        value = value.astype(BF16)
        for i in range(block // rows):
            if offsets is None:
                target = out_refs[0].at[first // rows + i]
            else:
                target = out_refs[offsets[i] % 2].at[offsets[i] // 2]
            target[:, at] = value[i * rows : (i + 1) * rows]

    def one_block(first):
        tops, totals = [], []
        for pair in range(width // PAIR):
            if pieces == 1:
                query = piece_refs[0][pl.ds(first, block), columns(pair)]
            else:
                query = stacked(piece_refs, columns(pair))
            out, total, (low, high) = attend_pair(
                query, key_ref[:, columns(pair)], value_ref[:, columns(pair)], round_up
            )
            put(first, columns(pair), out)
            lane = lax.broadcasted_iota(jnp.int32, (block, PAIR), 1)
            tops.append(jnp.where(lane < HEAD_DIM, low, high))
            totals.append(total)
        put(first, slice(width, width + PAIR), statistics(tops, totals))

    if block == queries:
        one_block(0)
    else:
        pl.loop(0, queries // block)(lambda i: one_block(pl.multiple_of(i * block, block)))


def audio_part(pieces, offsets, video_k, video_v, rows, size):
    keys, width = video_k.shape
    work = rows * size * keys * width
    assert width // PAIR <= 8
    shapes = [(size, rows, width + PAIR)] if offsets is None else [(size // 2, rows, width + PAIR)] * 2
    return pl.pallas_call(
        functools.partial(audio_kernel, pieces=len(pieces), offsets=offsets),
        out_shape=[pltpu.VMEM(shape, BF16) for shape in shapes],
        in_specs=[VMEM] * (2 + len(pieces)),
        out_specs=[VMEM] * len(shapes),
        compiler_params=pltpu.CompilerParams(vmem_limit_bytes=24 << 20),
        cost_estimate=pl.CostEstimate(
            flops=4 * work,
            bytes_accessed=4 * keys * width,
            transcendentals=work // HEAD_DIM,
        ),
        name="audio_part",
    )(*pieces, video_k, video_v)


def joined(part_refs):
    width = part_refs[0].shape[1] - PAIR
    at = lax.broadcasted_iota(jnp.int32, (PAIR, width), 0)
    head = lax.broadcasted_iota(jnp.int32, (PAIR, width), 1) // HEAD_DIM
    home = (head % 2) * HEAD_DIM + (head // 2) * 8
    pick_top = (at == home).astype(BF16)
    pick_total = ((at == home + 3) | (at == home + 6)).astype(BF16)
    stats = [ref[:, pl.ds(width, PAIR)] for ref in part_refs]
    tops = [jnp.dot(s, pick_top, preferred_element_type=F32) for s in stats]
    totals = [jnp.dot(s, pick_total, preferred_element_type=F32) for s in stats]
    top = functools.reduce(jnp.maximum, tops)
    total, out = 0.0, 0.0
    for i, ref in enumerate(part_refs):
        factor = jnp.exp(tops[i] - top)
        total = total + factor * totals[i]
        out = out + factor * ref[:, pl.ds(0, width)].astype(F32)
    return out, total, top


def merge_kernel(mine_ref, theirs_ref, *out_refs):
    for i, out_ref in enumerate(out_refs):
        out, total, top = joined([mine_ref.at[i], theirs_ref.at[i]])
        width = out.shape[1]
        out_ref[:, pl.ds(0, width)] = out.astype(BF16)
        pairs = [columns(pair) for pair in range(width // PAIR)]
        stats = statistics([top[:, at] for at in pairs], [total[:, at] for at in pairs])
        out_ref[:, pl.ds(width, PAIR)] = stats.astype(BF16)


def merge(mine, theirs):
    owners, rows, wide = mine.shape
    return pl.pallas_call(
        merge_kernel,
        out_shape=[pltpu.VMEM((rows, wide), BF16)] * owners,
        in_specs=[VMEM] * 2,
        out_specs=[VMEM] * owners,
        compiler_params=pltpu.CompilerParams(vmem_limit_bytes=8 << 20),
        name="audio_merge",
    )(mine, theirs)


def finish_kernel(gain_ref, *refs, parts, steps, axis, size):
    part_refs, refs = refs[:parts], refs[parts:]
    *block_refs, audio_ref, video_ref, audio_done, video_done, audio_sem, sems = refs
    if len(part_refs[0].shape) == 3:
        part_refs = [part_refs[0].at[i] for i in range(part_refs[0].shape[0])]
    out, total, _ = joined(part_refs)
    audio_done[...] = (out / total).astype(BF16)
    copies = [pltpu.make_async_copy(audio_done, audio_ref, audio_sem)]
    copies[0].start()

    rows, width = block_refs[0].shape
    me = lax.axis_index(axis)
    count = rows // sems.shape[0]
    for i in range(sems.shape[0]):
        here = pl.ds(i * count, count)
        square = 0.0
        for block_ref in block_refs:
            block = block_ref[here, :].astype(F32)
            square = square + jnp.sum(block * block, axis=1, keepdims=True)
        factor = lax.rsqrt(square / video_ref.shape[1] + 1e-06)
        for step, block_ref in zip(steps, block_refs):
            owner = me if step == 0 else sender(me, step, size)
            at = pl.ds(pl.multiple_of(owner * width, width), width)
            block = block_ref[here, :].astype(F32)
            video_done[here, at] = (block * factor * gain_ref[:, at]).astype(BF16)
        copies.append(pltpu.make_async_copy(video_done.at[here], video_ref.at[here], sems.at[i]))
        copies[-1].start()
    for copy in copies:
        copy.wait()


def finish(gain, parts, blocks, steps, size):
    audio_rows, wide = parts[0].shape[-2:]
    rows, width = blocks[0].shape
    cuts = next(n for n in (7, 4, 2, 1) if rows % (16 * n) == 0 or n == 1)
    shapes = [(audio_rows, wide - PAIR), (rows, width * size)]
    return pl.pallas_call(
        functools.partial(finish_kernel, parts=len(parts), steps=steps, axis="head", size=size),
        out_shape=[jax.ShapeDtypeStruct(shape, BF16) for shape in shapes],
        in_specs=[VMEM] * (1 + len(parts) + len(blocks)),
        out_specs=[pl.BlockSpec(memory_space=pltpu.HBM)] * 2,
        scratch_shapes=[pltpu.VMEM(shape, BF16) for shape in shapes]
        + [pltpu.SemaphoreType.DMA(()), pltpu.SemaphoreType.DMA((cuts,))],
        compiler_params=pltpu.CompilerParams(vmem_limit_bytes=12 << 20),
        name="finish",
    )(gain.reshape(1, -1), *parts, *blocks)


def is_direct(size):
    return size & (size - 1) == 0 and 2 <= size <= DIRECT_LIMIT


def gather(x, axis):
    size = lax.axis_size(axis)
    if not is_direct(size):
        return [lax.all_gather(x, axis, axis=0, tiled=True)], None
    pieces = {0: x}
    out, beside = gather_steps(size)
    for step in out:
        pieces[step] = exchange(x, axis, step)
    for step in beside:
        pieces[step] = exchange(pieces[step - 1], axis, 1)
    return list(pieces.values()), list(pieces)


def attend_all(video_q, video_k, video_v, audio_q, audio_k, audio_v, norm_gain):
    heads, toks = lax.axis_size("head"), lax.axis_size("tok")
    rows, audio_rows = video_q.shape[0] // heads, audio_q.shape[0]
    early, *late = partners(heads)

    own, keys = pack(audio_q, audio_k, audio_v)
    keys = exchange(keys, "head", early)
    video_q, block = stage(video_q, early, heads)
    keys, block = lax.optimization_barrier((keys, block))
    block = exchange(block, "head", early)
    pieces, offsets = gather(own, "tok")
    other_pieces, _ = gather(keys, "tok")

    received = []
    for step in late:
        piece = video_part(video_q, pieces, rows, step, heads)
        received.append(exchange(piece, "head", step))
    mine = video_part(video_q, pieces, rows, 0, heads)
    came = video_part(block, other_pieces, rows, early, heads)
    parts = audio_part(pieces, offsets, video_k, video_v, audio_rows, toks)
    if offsets is None:
        parts = lax.all_to_all(parts[0], "tok", split_axis=0, concat_axis=0, tiled=True)
        parts = [parts]
    else:
        theirs = exchange(parts[1], "tok", 1)
        merged = merge(parts[0], theirs)
        parts = list(merged[:1])
        for step in gather_steps(toks)[0][:-1]:
            parts.append(exchange(merged[step // 2], "tok", step))
    blocks = [mine, came, *received]
    audio_out, video_out = finish(norm_gain, parts, blocks, [0, early, *late], heads)
    return (video_out, audio_out)


def gather_steps(size):
    steps = sorted(range(2, size, 2), key=lambda s: (-s.bit_count(), -s))
    return [*steps, 1], [s + 1 for s in steps]


def solution(mesh):
    placed = P("tok", "head")
    return jax.shard_map(
        attend_all,
        mesh=mesh,
        in_specs=(placed,) * 6 + (P(),),
        out_specs=(P(("tok", "head"), None), placed),
        check_vma=False,
    )
```

```python
import functools

import jax
import jax.numpy as jnp
from jax import lax
from jax.experimental import pallas as pl
from jax.experimental.pallas import tpu as pltpu
from jax.sharding import PartitionSpec as P


HEAD_DIM = 64
PAIR = 2 * HEAD_DIM
QUERY_BLOCK = 256
DIRECT_LIMIT = 8
BF16, F32 = jnp.bfloat16, jnp.float32
VMEM = pl.BlockSpec(memory_space=pltpu.VMEM)


def partners(size):
    steps = sorted(range(1, size), key=lambda s: (-s.bit_length(), s))
    return steps if size & (size - 1) == 0 else list(range(1, size))


def peer(me, step, size):
    return me ^ step if size & (size - 1) == 0 else lax.rem(me + step, size)


def sender(me, step, size):
    return me ^ step if size & (size - 1) == 0 else lax.rem(me + size - step, size)


def exchange(x, axis, step):
    size = lax.axis_size(axis)
    pairs = [
        (i, i ^ step if size & (size - 1) == 0 else (i + step) % size)
        for i in range(size)
    ]
    return lax.ppermute(x, axis, pairs)


def columns(pair, base=0):
    return slice(base + pair * PAIR, base + (pair + 1) * PAIR)


def lane_halves(x):
    lane = lax.broadcasted_iota(jnp.int32, x.shape, 1)
    zero = jnp.zeros_like(x)
    return jnp.where(lane < HEAD_DIM, x, zero), jnp.where(lane < HEAD_DIM, zero, x)


def attend_pair(query, key, value, shift_of):
    query = query * HEAD_DIM**-0.5
    weights, shifts = [], []
    for one in lane_halves(key):
        scores = lax.dot_general(
            query, one, (((1,), (1,)), ((), ())), preferred_element_type=F32
        )
        shift = shift_of(jnp.max(scores, axis=1, keepdims=True))
        weights.append(jnp.exp(scores - shift).astype(BF16))
        shifts.append(shift)
    result = None
    for weight, v, one in zip(weights, lane_halves(value), lane_halves(jnp.ones_like(value))):
        part = jnp.dot(
            weight, jnp.concatenate([v, one], axis=1), preferred_element_type=F32
        )
        result = part if result is None else result + part
    return result[:, :PAIR], result[:, PAIR:], shifts


def copy_all(pairs, sems):
    copies = [
        pltpu.make_async_copy(source, target, sems.at[i])
        for i, (source, target) in enumerate(pairs)
    ]
    for copy in copies:
        copy.start()
    for copy in copies:
        copy.wait()


def pack_kernel(q_ref, k_ref, v_ref, video_ref, own_ref, keys_ref, block_ref, sems, *, step, size):
    rows, width = block_ref.shape
    first = pl.multiple_of(peer(lax.axis_index("head"), step, size) * rows, rows)
    spots = [(own_ref, 0, q_ref), (own_ref, 1, k_ref), (own_ref, 2, v_ref)]
    spots += [(keys_ref, 0, k_ref), (keys_ref, 1, v_ref)]
    spots = [(part, target.at[:, pl.ds(i * width, width)]) for target, i, part in spots]
    copy_all([(video_ref.at[pl.ds(first, rows)], block_ref), *spots], sems)


def in_hbm(*arrays):
    return [pltpu.with_memory_space_constraint(x, pltpu.HBM) for x in arrays]


def pack(audio_q, audio_k, audio_v, video_q, step, size):
    audio_rows, width = audio_q.shape
    shapes = [(audio_rows, 3 * width), (audio_rows, 2 * width), (video_q.shape[0] // size, width)]
    return pl.pallas_call(
        functools.partial(pack_kernel, step=step, size=size),
        out_shape=[pltpu.VMEM(shape, BF16) for shape in shapes],
        in_specs=[pl.BlockSpec(memory_space=pltpu.HBM)] * 4,
        out_specs=[VMEM] * 3,
        scratch_shapes=[pltpu.SemaphoreType.DMA((6,))],
        compiler_params=pltpu.CompilerParams(vmem_limit_bytes=8 << 20),
        name="pack",
    )(*in_hbm(audio_q, audio_k, audio_v, video_q))


def stacked(refs, at):
    return jnp.concatenate([ref[:, at] for ref in refs], axis=0)


def video_kernel(query_ref, *refs, step, axis, size, base):
    *piece_refs, out_ref = refs
    rows, width = out_ref.shape
    first = 0
    if query_ref.shape[0] != rows:
        me = lax.axis_index(axis)
        owner = me if step == 0 else peer(me, step, size)
        first = pl.multiple_of(owner * rows, rows)
    for pair in range(width // PAIR):
        out, total, _ = attend_pair(
            query_ref[pl.ds(first, rows), columns(pair)],
            stacked(piece_refs, columns(pair, base)),
            stacked(piece_refs, columns(pair, base + width)),
            lambda top: top,
        )
        out_ref[:, columns(pair)] = (out / total).astype(BF16)


def video_part(query, pieces, rows, step, size):
    width = query.shape[1]
    base = pieces[0].shape[1] - 2 * width
    work = rows * sum(piece.shape[0] for piece in pieces) * width
    return pl.pallas_call(
        functools.partial(
            video_kernel, step=step, axis="head", size=size, base=base
        ),
        out_shape=pltpu.VMEM((rows, width), BF16),
        in_specs=[VMEM] * (1 + len(pieces)),
        out_specs=VMEM,
        compiler_params=pltpu.CompilerParams(vmem_limit_bytes=16 << 20),
        cost_estimate=pl.CostEstimate(
            flops=4 * work,
            bytes_accessed=4 * rows * width,
            transcendentals=work // HEAD_DIM,
        ),
        name="video_part",
    )(query, *pieces)


def round_up(top):
    return (top + jnp.abs(top) * 2.0**-8).astype(BF16).astype(F32)


def statistics(tops, totals):
    lane = lax.broadcasted_iota(jnp.int32, tops[0].shape, 1)
    top, total = jnp.zeros(lane.shape, F32), jnp.zeros(lane.shape, F32)
    for pair in range(len(tops)):
        mine = (lane % HEAD_DIM) // 8 == pair
        top = jnp.where(mine, tops[pair], top)
        total = jnp.where(mine, totals[pair], total)
    coarse = total.astype(BF16).astype(F32)
    kind = lane % 8
    return jnp.where(kind < 3, top, jnp.where(kind < 6, coarse, total - coarse))


def audio_kernel(*refs, pieces, offsets):
    piece_refs, (key_ref, value_ref, *out_refs) = refs[:pieces], refs[pieces:]
    rows = out_refs[0].shape[1]
    width = key_ref.shape[1]
    queries = sum(ref.shape[0] for ref in piece_refs)
    block = queries
    if pieces == 1 and queries % QUERY_BLOCK == 0 and QUERY_BLOCK % rows == 0:
        block = QUERY_BLOCK

    def put(first, at, value):
        value = value.astype(BF16)
        for i in range(block // rows):
            if offsets is None:
                target = out_refs[0].at[first // rows + i]
            else:
                target = out_refs[offsets[i] % 2].at[offsets[i] // 2]
            target[:, at] = value[i * rows : (i + 1) * rows]

    def one_block(first):
        tops, totals = [], []
        for pair in range(width // PAIR):
            if pieces == 1:
                query = piece_refs[0][pl.ds(first, block), columns(pair)]
            else:
                query = stacked(piece_refs, columns(pair))
            out, total, (low, high) = attend_pair(
                query, key_ref[:, columns(pair)], value_ref[:, columns(pair)], round_up
            )
            put(first, columns(pair), out)
            lane = lax.broadcasted_iota(jnp.int32, (block, PAIR), 1)
            tops.append(jnp.where(lane < HEAD_DIM, low, high))
            totals.append(total)
        put(first, slice(width, width + PAIR), statistics(tops, totals))

    if block == queries:
        one_block(0)
    else:
        pl.loop(0, queries // block)(lambda i: one_block(pl.multiple_of(i * block, block)))


def audio_part(pieces, offsets, video_k, video_v, rows, size):
    keys, width = video_k.shape
    work = rows * size * keys * width
    assert width // PAIR <= 8
    shapes = [(size, rows, width + PAIR)] if offsets is None else [(size // 2, rows, width + PAIR)] * 2
    return pl.pallas_call(
        functools.partial(audio_kernel, pieces=len(pieces), offsets=offsets),
        out_shape=[pltpu.VMEM(shape, BF16) for shape in shapes],
        in_specs=[VMEM] * (2 + len(pieces)),
        out_specs=[VMEM] * len(shapes),
        compiler_params=pltpu.CompilerParams(vmem_limit_bytes=24 << 20),
        cost_estimate=pl.CostEstimate(
            flops=4 * work,
            bytes_accessed=4 * keys * width,
            transcendentals=work // HEAD_DIM,
        ),
        name="audio_part",
    )(*pieces, video_k, video_v)


def joined(part_refs):
    width = part_refs[0].shape[1] - PAIR
    at = lax.broadcasted_iota(jnp.int32, (PAIR, width), 0)
    head = lax.broadcasted_iota(jnp.int32, (PAIR, width), 1) // HEAD_DIM
    home = (head % 2) * HEAD_DIM + (head // 2) * 8
    pick_top = (at == home).astype(BF16)
    pick_total = ((at == home + 3) | (at == home + 6)).astype(BF16)
    stats = [ref[:, pl.ds(width, PAIR)] for ref in part_refs]
    tops = [jnp.dot(s, pick_top, preferred_element_type=F32) for s in stats]
    totals = [jnp.dot(s, pick_total, preferred_element_type=F32) for s in stats]
    top = functools.reduce(jnp.maximum, tops)
    total, out = 0.0, 0.0
    for i, ref in enumerate(part_refs):
        factor = jnp.exp(tops[i] - top)
        total = total + factor * totals[i]
        out = out + factor * ref[:, pl.ds(0, width)].astype(F32)
    return out, total, top


def merge_kernel(mine_ref, theirs_ref, *out_refs):
    for i, out_ref in enumerate(out_refs):
        out, total, top = joined([mine_ref.at[i], theirs_ref.at[i]])
        width = out.shape[1]
        out_ref[:, pl.ds(0, width)] = out.astype(BF16)
        pairs = [columns(pair) for pair in range(width // PAIR)]
        stats = statistics([top[:, at] for at in pairs], [total[:, at] for at in pairs])
        out_ref[:, pl.ds(width, PAIR)] = stats.astype(BF16)


def merge(mine, theirs):
    owners, rows, wide = mine.shape
    return pl.pallas_call(
        merge_kernel,
        out_shape=[pltpu.VMEM((rows, wide), BF16)] * owners,
        in_specs=[VMEM] * 2,
        out_specs=[VMEM] * owners,
        compiler_params=pltpu.CompilerParams(vmem_limit_bytes=8 << 20),
        name="audio_merge",
    )(mine, theirs)


def finish_kernel(gain_ref, *refs, parts, steps, axis, size):
    part_refs, refs = refs[:parts], refs[parts:]
    *block_refs, audio_ref, video_ref, audio_done, video_done, audio_sem, sems = refs
    if len(part_refs[0].shape) == 3:
        part_refs = [part_refs[0].at[i] for i in range(part_refs[0].shape[0])]
    out, total, _ = joined(part_refs)
    audio_done[...] = (out / total).astype(BF16)
    copies = [pltpu.make_async_copy(audio_done, audio_ref, audio_sem)]
    copies[0].start()

    rows, width = block_refs[0].shape
    me = lax.axis_index(axis)
    count = rows // sems.shape[0]
    for i in range(sems.shape[0]):
        here = pl.ds(i * count, count)
        square = 0.0
        for block_ref in block_refs:
            block = block_ref[here, :].astype(F32)
            square = square + jnp.sum(block * block, axis=1, keepdims=True)
        factor = lax.rsqrt(square / video_ref.shape[1] + 1e-06)
        for step, block_ref in zip(steps, block_refs):
            owner = me if step == 0 else sender(me, step, size)
            at = pl.ds(pl.multiple_of(owner * width, width), width)
            block = block_ref[here, :].astype(F32)
            video_done[here, at] = (block * factor * gain_ref[:, at]).astype(BF16)
        copies.append(pltpu.make_async_copy(video_done.at[here], video_ref.at[here], sems.at[i]))
        copies[-1].start()
    for copy in copies:
        copy.wait()


def finish(gain, parts, blocks, steps, size):
    audio_rows, wide = parts[0].shape[-2:]
    rows, width = blocks[0].shape
    cuts = next(n for n in (7, 4, 2, 1) if rows % (16 * n) == 0 or n == 1)
    shapes = [(audio_rows, wide - PAIR), (rows, width * size)]
    return pl.pallas_call(
        functools.partial(finish_kernel, parts=len(parts), steps=steps, axis="head", size=size),
        out_shape=[jax.ShapeDtypeStruct(shape, BF16) for shape in shapes],
        in_specs=[VMEM] * (1 + len(parts) + len(blocks)),
        out_specs=[pl.BlockSpec(memory_space=pltpu.HBM)] * 2,
        scratch_shapes=[pltpu.VMEM(shape, BF16) for shape in shapes]
        + [pltpu.SemaphoreType.DMA(()), pltpu.SemaphoreType.DMA((cuts,))],
        compiler_params=pltpu.CompilerParams(vmem_limit_bytes=12 << 20),
        name="finish",
    )(gain.reshape(1, -1), *parts, *blocks)


def is_direct(size):
    return size & (size - 1) == 0 and 2 <= size <= DIRECT_LIMIT


def gather(x, axis):
    size = lax.axis_size(axis)
    if not is_direct(size):
        return [lax.all_gather(x, axis, axis=0, tiled=True)], None
    pieces = {0: x}
    out, beside = gather_steps(size)
    for step in out:
        pieces[step] = exchange(x, axis, step)
    for step in beside:
        pieces[step] = exchange(pieces[step - 1], axis, 1)
    return list(pieces.values()), list(pieces)


def attend_all(video_q, video_k, video_v, audio_q, audio_k, audio_v, norm_gain):
    heads, toks = lax.axis_size("head"), lax.axis_size("tok")
    rows, audio_rows = video_q.shape[0] // heads, audio_q.shape[0]
    early, *late = partners(heads)

    own, keys, block = pack(audio_q, audio_k, audio_v, video_q, early, heads)
    keys = exchange(keys, "head", early)
    keys, block = lax.optimization_barrier((keys, block))
    block = exchange(block, "head", early)
    pieces, offsets = gather(own, "tok")
    other_pieces, _ = gather(keys, "tok")

    received = []
    for step in late:
        piece = video_part(video_q, pieces, rows, step, heads)
        received.append(exchange(piece, "head", step))
    mine = video_part(video_q, pieces, rows, 0, heads)
    came = video_part(block, other_pieces, rows, early, heads)
    parts = audio_part(pieces, offsets, video_k, video_v, audio_rows, toks)
    if offsets is None:
        parts = lax.all_to_all(parts[0], "tok", split_axis=0, concat_axis=0, tiled=True)
        parts = [parts]
    else:
        theirs = exchange(parts[1], "tok", 1)
        merged = merge(parts[0], theirs)
        parts = list(merged[:1])
        for step in gather_steps(toks)[0][:-1]:
            parts.append(exchange(merged[step // 2], "tok", step))
    blocks = [mine, came, *received]
    audio_out, video_out = finish(norm_gain, parts, blocks, [0, early, *late], heads)
    return (video_out, audio_out)


def gather_steps(size):
    steps = sorted(range(2, size, 2), key=lambda s: (-s.bit_count(), -s))
    return [*steps, 1], [s + 1 for s in steps]


def solution(mesh):
    placed = P("tok", "head")
    return jax.shard_map(
        attend_all,
        mesh=mesh,
        in_specs=(placed,) * 6 + (P(),),
        out_specs=(P(("tok", "head"), None), placed),
        check_vma=False,
    )
```

```python
import functools

import jax
import jax.numpy as jnp
from jax import lax
from jax.experimental import pallas as pl
from jax.experimental.pallas import tpu as pltpu
from jax.sharding import PartitionSpec as P


HEAD_DIM = 64
PAIR = 2 * HEAD_DIM
QUERY_BLOCK = 256
DIRECT_LIMIT = 8
BF16, F32 = jnp.bfloat16, jnp.float32
VMEM = pl.BlockSpec(memory_space=pltpu.VMEM)


def partners(size):
    steps = sorted(range(1, size), key=lambda s: (-s.bit_length(), -s))
    return steps if size & (size - 1) == 0 else list(range(1, size))


def peer(me, step, size):
    return me ^ step if size & (size - 1) == 0 else lax.rem(me + step, size)


def sender(me, step, size):
    return me ^ step if size & (size - 1) == 0 else lax.rem(me + size - step, size)


def exchange(x, axis, step):
    size = lax.axis_size(axis)
    pairs = [
        (i, i ^ step if size & (size - 1) == 0 else (i + step) % size)
        for i in range(size)
    ]
    return lax.ppermute(x, axis, pairs)


def columns(pair, base=0):
    return slice(base + pair * PAIR, base + (pair + 1) * PAIR)


def lane_halves(x):
    lane = lax.broadcasted_iota(jnp.int32, x.shape, 1)
    zero = jnp.zeros_like(x)
    return jnp.where(lane < HEAD_DIM, x, zero), jnp.where(lane < HEAD_DIM, zero, x)


def attend_pair(query, key, value, shift_of):
    rows = query.shape[0]
    query = query * HEAD_DIM**-0.5
    scores = lax.dot_general(
        jnp.concatenate(lane_halves(query), axis=0),
        key,
        (((1,), (1,)), ((), ())),
        preferred_element_type=F32,
    )
    shift = shift_of(jnp.max(scores, axis=1, keepdims=True))
    weights = jnp.exp(scores - shift).astype(BF16)
    result = jnp.dot(
        weights,
        jnp.concatenate([value, jnp.ones_like(value)], axis=1),
        preferred_element_type=F32,
    )
    lane = lax.broadcasted_iota(jnp.int32, (rows, 2 * PAIR), 1)
    result = jnp.where(lane % PAIR < HEAD_DIM, result[:rows], result[rows:])
    return result[:, :PAIR], result[:, PAIR:], (shift[:rows], shift[rows:])


def copy_all(pairs, sems):
    copies = [
        pltpu.make_async_copy(source, target, sems.at[i])
        for i, (source, target) in enumerate(pairs)
    ]
    for copy in copies:
        copy.start()
    for copy in copies:
        copy.wait()


def pack_kernel(q_ref, k_ref, v_ref, video_ref, own_ref, keys_ref, block_ref, sems, *, step, size):
    rows, width = block_ref.shape
    first = pl.multiple_of(peer(lax.axis_index("head"), step, size) * rows, rows)
    spots = [(own_ref, 0, q_ref), (own_ref, 1, k_ref), (own_ref, 2, v_ref)]
    spots += [(keys_ref, 0, k_ref), (keys_ref, 1, v_ref)]
    spots = [(part, target.at[:, pl.ds(i * width, width)]) for target, i, part in spots]
    copy_all([(video_ref.at[pl.ds(first, rows)], block_ref), *spots], sems)


def in_hbm(*arrays):
    return [pltpu.with_memory_space_constraint(x, pltpu.HBM) for x in arrays]


def pack(audio_q, audio_k, audio_v, video_q, step, size):
    audio_rows, width = audio_q.shape
    shapes = [(audio_rows, 3 * width), (audio_rows, 2 * width), (video_q.shape[0] // size, width)]
    return pl.pallas_call(
        functools.partial(pack_kernel, step=step, size=size),
        out_shape=[pltpu.VMEM(shape, BF16) for shape in shapes],
        in_specs=[pl.BlockSpec(memory_space=pltpu.HBM)] * 4,
        out_specs=[VMEM] * 3,
        scratch_shapes=[pltpu.SemaphoreType.DMA((6,))],
        compiler_params=pltpu.CompilerParams(vmem_limit_bytes=8 << 20),
        name="pack",
    )(*in_hbm(audio_q, audio_k, audio_v, video_q))


def stacked(refs, at):
    return jnp.concatenate([ref[:, at] for ref in refs], axis=0)


def video_kernel(query_ref, *refs, step, axis, size, base):
    *piece_refs, out_ref = refs
    rows, width = out_ref.shape
    first = 0
    if query_ref.shape[0] != rows:
        me = lax.axis_index(axis)
        owner = me if step == 0 else peer(me, step, size)
        first = pl.multiple_of(owner * rows, rows)
    for pair in range(width // PAIR):
        out, total, _ = attend_pair(
            query_ref[pl.ds(first, rows), columns(pair)],
            stacked(piece_refs, columns(pair, base)),
            stacked(piece_refs, columns(pair, base + width)),
            lambda top: top,
        )
        out_ref[:, columns(pair)] = (out / total).astype(BF16)


def video_part(query, pieces, rows, step, size):
    width = query.shape[1]
    base = pieces[0].shape[1] - 2 * width
    work = rows * sum(piece.shape[0] for piece in pieces) * width
    return pl.pallas_call(
        functools.partial(
            video_kernel, step=step, axis="head", size=size, base=base
        ),
        out_shape=pltpu.VMEM((rows, width), BF16),
        in_specs=[VMEM] * (1 + len(pieces)),
        out_specs=VMEM,
        compiler_params=pltpu.CompilerParams(vmem_limit_bytes=16 << 20),
        cost_estimate=pl.CostEstimate(
            flops=4 * work,
            bytes_accessed=4 * rows * width,
            transcendentals=work // HEAD_DIM,
        ),
        name="video_part",
    )(query, *pieces)


def round_up(top):
    return (top + jnp.abs(top) * 2.0**-8).astype(BF16).astype(F32)


def statistics(tops, totals):
    lane = lax.broadcasted_iota(jnp.int32, tops[0].shape, 1)
    top, total = jnp.zeros(lane.shape, F32), jnp.zeros(lane.shape, F32)
    for pair in range(len(tops)):
        mine = (lane % HEAD_DIM) // 8 == pair
        top = jnp.where(mine, tops[pair], top)
        total = jnp.where(mine, totals[pair], total)
    coarse = total.astype(BF16).astype(F32)
    kind = lane % 8
    return jnp.where(kind < 3, top, jnp.where(kind < 6, coarse, total - coarse))


def audio_kernel(*refs, pieces, offsets):
    piece_refs, (key_ref, value_ref, *out_refs) = refs[:pieces], refs[pieces:]
    rows = out_refs[0].shape[1]
    width = key_ref.shape[1]
    queries = sum(ref.shape[0] for ref in piece_refs)
    block = queries
    if pieces == 1 and queries % QUERY_BLOCK == 0 and QUERY_BLOCK % rows == 0:
        block = QUERY_BLOCK

    def put(first, at, value):
        value = value.astype(BF16)
        for i in range(block // rows):
            if offsets is None:
                target = out_refs[0].at[first // rows + i]
            else:
                target = out_refs[offsets[i] % 2].at[offsets[i] // 2]
            target[:, at] = value[i * rows : (i + 1) * rows]

    def one_block(first):
        tops, totals = [], []
        for pair in range(width // PAIR):
            if pieces == 1:
                query = piece_refs[0][pl.ds(first, block), columns(pair)]
            else:
                query = stacked(piece_refs, columns(pair))
            out, total, (low, high) = attend_pair(
                query, key_ref[:, columns(pair)], value_ref[:, columns(pair)], round_up
            )
            put(first, columns(pair), out)
            lane = lax.broadcasted_iota(jnp.int32, (block, PAIR), 1)
            tops.append(jnp.where(lane < HEAD_DIM, low, high))
            totals.append(total)
        put(first, slice(width, width + PAIR), statistics(tops, totals))

    if block == queries:
        one_block(0)
    else:
        pl.loop(0, queries // block)(lambda i: one_block(pl.multiple_of(i * block, block)))


def audio_part(pieces, offsets, video_k, video_v, rows, size):
    keys, width = video_k.shape
    work = rows * size * keys * width
    assert width // PAIR <= 8
    shapes = [(size, rows, width + PAIR)] if offsets is None else [(size // 2, rows, width + PAIR)] * 2
    return pl.pallas_call(
        functools.partial(audio_kernel, pieces=len(pieces), offsets=offsets),
        out_shape=[pltpu.VMEM(shape, BF16) for shape in shapes],
        in_specs=[VMEM] * (2 + len(pieces)),
        out_specs=[VMEM] * len(shapes),
        compiler_params=pltpu.CompilerParams(vmem_limit_bytes=24 << 20),
        cost_estimate=pl.CostEstimate(
            flops=4 * work,
            bytes_accessed=4 * keys * width,
            transcendentals=work // HEAD_DIM,
        ),
        name="audio_part",
    )(*pieces, video_k, video_v)


def joined(part_refs):
    width = part_refs[0].shape[1] - PAIR
    at = lax.broadcasted_iota(jnp.int32, (PAIR, width), 0)
    head = lax.broadcasted_iota(jnp.int32, (PAIR, width), 1) // HEAD_DIM
    home = (head % 2) * HEAD_DIM + (head // 2) * 8
    pick_top = (at == home).astype(BF16)
    pick_total = ((at == home + 3) | (at == home + 6)).astype(BF16)
    stats = [ref[:, pl.ds(width, PAIR)] for ref in part_refs]
    tops = [jnp.dot(s, pick_top, preferred_element_type=F32) for s in stats]
    totals = [jnp.dot(s, pick_total, preferred_element_type=F32) for s in stats]
    top = functools.reduce(jnp.maximum, tops)
    total, out = 0.0, 0.0
    for i, ref in enumerate(part_refs):
        factor = jnp.exp(tops[i] - top)
        total = total + factor * totals[i]
        out = out + factor * ref[:, pl.ds(0, width)].astype(F32)
    return out, total, top


def merge_kernel(mine_ref, theirs_ref, *out_refs):
    for i, out_ref in enumerate(out_refs):
        out, total, top = joined([mine_ref.at[i], theirs_ref.at[i]])
        width = out.shape[1]
        out_ref[:, pl.ds(0, width)] = out.astype(BF16)
        pairs = [columns(pair) for pair in range(width // PAIR)]
        stats = statistics([top[:, at] for at in pairs], [total[:, at] for at in pairs])
        out_ref[:, pl.ds(width, PAIR)] = stats.astype(BF16)


def merge(mine, theirs):
    owners, rows, wide = mine.shape
    return pl.pallas_call(
        merge_kernel,
        out_shape=[pltpu.VMEM((rows, wide), BF16)] * owners,
        in_specs=[VMEM] * 2,
        out_specs=[VMEM] * owners,
        compiler_params=pltpu.CompilerParams(vmem_limit_bytes=8 << 20),
        name="audio_merge",
    )(mine, theirs)


def finish_kernel(gain_ref, *refs, parts, steps, axis, size):
    part_refs, refs = refs[:parts], refs[parts:]
    *block_refs, audio_ref, video_ref, audio_done, video_done, audio_sem, sems = refs
    if len(part_refs[0].shape) == 3:
        part_refs = [part_refs[0].at[i] for i in range(part_refs[0].shape[0])]
    out, total, _ = joined(part_refs)
    audio_done[...] = (out / total).astype(BF16)
    copies = [pltpu.make_async_copy(audio_done, audio_ref, audio_sem)]
    copies[0].start()

    rows, width = block_refs[0].shape
    me = lax.axis_index(axis)
    count = rows // sems.shape[0]
    for i in range(sems.shape[0]):
        here = pl.ds(i * count, count)
        square = 0.0
        for block_ref in block_refs:
            block = block_ref[here, :].astype(F32)
            square = square + jnp.sum(block * block, axis=1, keepdims=True)
        factor = lax.rsqrt(square / video_ref.shape[1] + 1e-06)
        for step, block_ref in zip(steps, block_refs):
            owner = me if step == 0 else sender(me, step, size)
            at = pl.ds(pl.multiple_of(owner * width, width), width)
            block = block_ref[here, :].astype(F32)
            video_done[here, at] = (block * factor * gain_ref[:, at]).astype(BF16)
        copies.append(pltpu.make_async_copy(video_done.at[here], video_ref.at[here], sems.at[i]))
        copies[-1].start()
    for copy in copies:
        copy.wait()


def finish(gain, parts, blocks, steps, size):
    audio_rows, wide = parts[0].shape[-2:]
    rows, width = blocks[0].shape
    cuts = next(n for n in (7, 4, 2, 1) if rows % (16 * n) == 0 or n == 1)
    shapes = [(audio_rows, wide - PAIR), (rows, width * size)]
    return pl.pallas_call(
        functools.partial(finish_kernel, parts=len(parts), steps=steps, axis="head", size=size),
        out_shape=[jax.ShapeDtypeStruct(shape, BF16) for shape in shapes],
        in_specs=[VMEM] * (1 + len(parts) + len(blocks)),
        out_specs=[pl.BlockSpec(memory_space=pltpu.HBM)] * 2,
        scratch_shapes=[pltpu.VMEM(shape, BF16) for shape in shapes]
        + [pltpu.SemaphoreType.DMA(()), pltpu.SemaphoreType.DMA((cuts,))],
        compiler_params=pltpu.CompilerParams(vmem_limit_bytes=12 << 20),
        name="finish",
    )(gain.reshape(1, -1), *parts, *blocks)


def is_direct(size):
    return size & (size - 1) == 0 and 2 <= size <= DIRECT_LIMIT


def gather(x, axis):
    size = lax.axis_size(axis)
    if not is_direct(size):
        return [lax.all_gather(x, axis, axis=0, tiled=True)], None
    pieces = {0: x}
    out, beside = gather_steps(size)
    for step in out:
        pieces[step] = exchange(x, axis, step)
    for step in beside:
        pieces[step] = exchange(pieces[step - 1], axis, 1)
    return list(pieces.values()), list(pieces)


def attend_all(video_q, video_k, video_v, audio_q, audio_k, audio_v, norm_gain):
    heads, toks = lax.axis_size("head"), lax.axis_size("tok")
    rows, audio_rows = video_q.shape[0] // heads, audio_q.shape[0]
    early, *late = partners(heads)

    own, keys, block = pack(audio_q, audio_k, audio_v, video_q, early, heads)
    keys = exchange(keys, "head", early)
    keys, block = lax.optimization_barrier((keys, block))
    block = exchange(block, "head", early)
    pieces, offsets = gather(own, "tok")
    other_pieces, _ = gather(keys, "tok")

    received = []
    for step in late:
        piece = video_part(video_q, pieces, rows, step, heads)
        received.append(exchange(piece, "head", step))
    mine = video_part(video_q, pieces, rows, 0, heads)
    came = video_part(block, other_pieces, rows, early, heads)
    parts = audio_part(pieces, offsets, video_k, video_v, audio_rows, toks)
    if offsets is None:
        parts = lax.all_to_all(parts[0], "tok", split_axis=0, concat_axis=0, tiled=True)
        parts = [parts]
    else:
        theirs = exchange(parts[1], "tok", 1)
        merged = merge(parts[0], theirs)
        parts = list(merged[:1])
        for step in gather_steps(toks)[0][:-1]:
            parts.append(exchange(merged[step // 2], "tok", step))
    blocks = [mine, came, *received]
    audio_out, video_out = finish(norm_gain, parts, blocks, [0, early, *late], heads)
    return (video_out, audio_out)


def gather_steps(size):
    steps = sorted(range(2, size, 2), key=lambda s: (-s.bit_count(), -s))
    return [*steps, 1], [s + 1 for s in steps]


def solution(mesh):
    placed = P("tok", "head")
    return jax.shard_map(
        attend_all,
        mesh=mesh,
        in_specs=(placed,) * 6 + (P(),),
        out_specs=(P(("tok", "head"), None), placed),
        check_vma=False,
    )
```
